512 devices in a mesh: gx: 16 (over y, z_hi, core), gy: 32 (over x, z_lo).
Axes of the slice: x: 4, y: 4, z: 16 (z_hi: 2, z_lo: 8; z = z_hi * 8 + z_lo), core: 2. Of those that a mesh axis runs over, the one named last changes fastest.
Arguments:
- tokens: bfloat16 [512, 16384], P('gy', 'gx'), may hold values from -6 to 6
- gate_weight: bfloat16 [16384, 26624], P('gx', 'gy'), may hold values from -0.046875 to 0.046875
- up_weight: bfloat16 [16384, 26624], P('gx', 'gy'), may hold values from -0.046875 to 0.046875
- down_weight: bfloat16 [26624, 16384], P('gy', 'gx'), may hold values from -0.0390625 to 0.0390625
Outputs:
- mixed: bfloat16 [512, 16384], P('gy', 'gx')
The draws below stay inside these ranges and needn't reach their ends.
All inputs are finite; a program needn't handle non-finite values.
Results may differ from the reference program's by a relative error of at most 0.0049.
Values may be sent and summed in bfloat16 or wider, within the bound.
No kernel may reach another device: no remote copies, remote signals or barrier semaphores. Data moves between devices by JAX's collectives and lax.ppermute only.
A program may use at most 64 MiB of HBM per device.

```python
import jax
import jax.numpy as jnp

D = 16384
FF = 26624
GROUP = 512


def level_of(rng, dims, pieces, smallest, top_value):
    def one(axis_at, shards_of):
        steps = jax.random.uniform(jax.random.fold_in(jax.random.fold_in(rng, 6), axis_at), (shards_of,), jnp.float32, smallest / len(pieces), top_value / len(pieces))
        return jnp.repeat(jnp.exp(steps), dims[axis_at] // shards_of).reshape((-1,) + (1,) * (len(dims) - axis_at - 1))

    gain = one(*pieces[0])
    for cut in pieces[1:]:
        gain = gain * one(*cut)
    return gain


def bell_draw(stream_key, extent, deviation, limit, cuts=(), kind=jnp.bfloat16):
    entries = deviation * jax.random.normal(stream_key, extent, jnp.float32)
    if cuts:
        entries = entries * level_of(stream_key, extent, cuts, -0.22, 0.18)
    return jnp.clip(entries, -limit, limit).astype(kind)


def setup_inputs(seed: int = 0) -> dict:
    seeds = jax.random.split(jax.random.key(seed), 5)
    tokens = bell_draw(seeds[0], (GROUP, D), 1.0, 6.0, ((0, 32), (1, 16)))
    gate_weight = bell_draw(seeds[1], (D, FF), D ** -0.5, 0.046875, ((0, 16), (1, 32)))
    up_weight = bell_draw(seeds[2], (D, FF), D ** -0.5, 0.046875, ((0, 16), (1, 32)))
    down_weight = bell_draw(seeds[3], (FF, D), FF ** -0.5, 0.0390625, ((0, 32), (1, 16)))
    return dict(tokens=tokens, gate_weight=gate_weight, up_weight=up_weight, down_weight=down_weight)


def reference(tokens, gate_weight, up_weight, down_weight):
    gate = jnp.dot(tokens, gate_weight, preferred_element_type=jnp.float32)
    up = jnp.dot(tokens, up_weight, preferred_element_type=jnp.float32)
    hidden = (jax.nn.silu(gate) * up).astype(jnp.bfloat16)
    mixed = jnp.dot(hidden, down_weight, preferred_element_type=jnp.float32)
    return mixed.astype(jnp.bfloat16)
```

```python
import jax
import jax.numpy as jnp
from jax import lax
from jax.experimental import pallas as pl
from jax.experimental.pallas import tpu as pltpu
from jax.sharding import Mesh, PartitionSpec as P

GX = (("y", 4), ("zh", 2), ("c", 2))
GY = (("x", 4), ("zl", 8))
BF = jnp.bfloat16
F32 = jnp.float32
SWAP = [(0, 1), (1, 0)]
VMEM = pl.BlockSpec(memory_space=pltpu.VMEM)
SMEM = pl.BlockSpec(memory_space=pltpu.SMEM)


def gather(value, axis, size):
    return lax.all_to_all(jnp.broadcast_to(value[None], (size,) + value.shape), axis, 0, 0)


def add_up(parts):
    total = parts[0].astype(F32)
    for i in range(1, parts.shape[0]):
        total = total + parts[i].astype(F32)
    return total


def gate_up_kernel(half_ref, x_ref, g_ref, u_ref, out_ref):
    n = x_ref.shape[0] // 2
    start = pl.multiple_of(half_ref[0] * n, n)
    x = x_ref[pl.ds(start, n), :]
    for i, w in enumerate((g_ref, u_ref)):
        part = lax.dot_general(x, w[...], (((1,), (1,)), ((), ())), preferred_element_type=F32)
        out_ref[:, i] = part.reshape(out_ref.shape[0], out_ref.shape[2], out_ref.shape[3])


def gate_up(half, x, g, u):
    tokens, hidden = x.shape[0], g.shape[0]
    return pl.pallas_call(
        gate_up_kernel,
        out_shape=jax.ShapeDtypeStruct((4, 2, tokens // 8, hidden), F32),
        in_specs=[SMEM, VMEM, VMEM, VMEM],
        out_specs=VMEM,
        cost_estimate=pl.CostEstimate(flops=2 * tokens * x.shape[1] * hidden, bytes_accessed=8 << 20, transcendentals=0),
        compiler_params=pltpu.CompilerParams(vmem_limit_bytes=16 << 20),
        name="gate_up",
    )(half, x, g, u)


def down_kernel(half_ref, mine_ref, far_ref, w_ref, out_ref):
    n = mine_ref.shape[0]
    for h, start in ((mine_ref, half_ref[0] * n), (far_ref, (1 - half_ref[0]) * n)):
        part = jnp.dot(h[...], w_ref[...], preferred_element_type=F32)
        out_ref[pl.ds(pl.multiple_of(start, n), n), :] = part.astype(BF)


def down(half, mine, far, w):
    n, hidden = mine.shape
    return pl.pallas_call(
        down_kernel,
        out_shape=jax.ShapeDtypeStruct((2 * n, w.shape[1]), BF),
        in_specs=[SMEM, VMEM, VMEM, VMEM],
        out_specs=VMEM,
        cost_estimate=pl.CostEstimate(flops=4 * n * hidden * w.shape[1], bytes_accessed=4 << 20, transcendentals=0),
        compiler_params=pltpu.CompilerParams(vmem_limit_bytes=16 << 20),
        name="down",
    )(half, mine, far, w)


def on_device(tokens, gate_weight, up_weight, down_weight):
    rows, width = tokens.shape
    hidden_units = gate_weight.shape[1]
    half = lax.axis_index("c").astype(jnp.int32).reshape(1)
    piece = gather(tokens, "zl", 8).reshape(8 * rows, width)
    piece = gather(piece, "x", 4).reshape(32 * rows, width)

    other = gate_up(1 - half, piece, gate_weight.T, up_weight.T)
    other = lax.ppermute(other, "c", SWAP)
    mine = gate_up(half, piece, gate_weight.T, up_weight.T)
    parts = lax.all_to_all((mine + other).astype(BF), "y", 0, 0)
    summed = add_up(parts)
    summed = summed + lax.ppermute(summed.astype(BF), "zh", SWAP).astype(F32)

    hidden = (jax.nn.silu(summed[0]) * summed[1]).astype(BF)
    hidden = gather(hidden, "y", 4).reshape(16 * rows, hidden_units)
    far = lax.ppermute(hidden, "c", SWAP)

    out = down(half, hidden, far, down_weight)
    out = add_up(lax.all_to_all(out.reshape(4, 8 * rows, width), "x", 0, 0))
    out = add_up(lax.all_to_all(out.reshape(8, rows, width), "zl", 0, 0))
    return out.astype(BF)


def solution(mesh):
    sizes = [n for _, n in GX + GY]
    names = [a for a, _ in GX + GY]
    fine = Mesh(mesh.devices.reshape(sizes), names)
    gx, gy = tuple(a for a, _ in GX), tuple(a for a, _ in GY)
    return jax.shard_map(
        on_device,
        mesh=fine,
        in_specs=(P(gy, gx), P(gx, gy), P(gx, gy), P(gy, gx)),
        out_specs=P(gy, gx),
        check_vma=False,
    )
```

```python
import jax
import jax.numpy as jnp
from jax import lax
from jax.experimental import pallas as pl
from jax.experimental.pallas import tpu as pltpu
from jax.sharding import Mesh, PartitionSpec as P

GX = (("y", 4), ("zh", 2), ("c", 2))
BF = jnp.bfloat16
F32 = jnp.float32
SWAP = [(0, 1), (1, 0)]
VMEM = pl.BlockSpec(memory_space=pltpu.VMEM)
SMEM = pl.BlockSpec(memory_space=pltpu.SMEM)
ZSPLIT = True
ZB, NB = ("zq", 4) if ZSPLIT else ("zl", 8)
XA = ("x", "zp") if ZSPLIT else "x"
GY = (("x", 4), ("zq", 4), ("zp", 2)) if ZSPLIT else (("x", 4), ("zl", 8))


def gather(value, axis, size):
    return lax.all_to_all(jnp.broadcast_to(value[None], (size,) + value.shape), axis, 0, 0)


def scatter_sum(terms, axis, me, own):
    terms, own = lax.optimization_barrier((terms, own))
    parts = lax.all_to_all(terms, axis, 0, 0)
    for part, far in zip(parts, me):
        own = own + jnp.where(far, part.astype(F32), 0.0)
    return own


def at(terms, me):
    return lax.dynamic_index_in_dim(terms, me, 0, keepdims=False, allow_negative_indices=False)


def gate_up_kernel(core_ref, x_ref, g_ref, u_ref, out_ref):
    y, _, rows, width = x_ref.shape
    x = x_ref[:, core_ref[0]].reshape(y * rows, width)
    for i, w in enumerate((g_ref, u_ref)):
        part = lax.dot_general(x, w[...], (((1,), (1,)), ((), ())), preferred_element_type=F32)
        n = part.shape[1]
        out_ref[:, :, i * n : (i + 1) * n] = part.reshape(y, rows, n)


def gate_up(core, x, g, u):
    y, _, rows, width = x.shape
    hidden = g.shape[0]
    return pl.pallas_call(
        gate_up_kernel,
        out_shape=jax.ShapeDtypeStruct((y, rows, 2 * hidden), F32),
        in_specs=[SMEM, VMEM, VMEM, VMEM],
        out_specs=VMEM,
        cost_estimate=pl.CostEstimate(flops=4 * y * rows * width * hidden, bytes_accessed=8 << 20, transcendentals=0),
        compiler_params=pltpu.CompilerParams(vmem_limit_bytes=16 << 20),
        name="gate_up",
    )(core, x, g, u)


def down_kernel(x_at_ref, h_ref, w_ref, out_ref, own_ref, sums):
    sums[...] = jnp.dot(h_ref[...], w_ref[...], preferred_element_type=F32)
    out_ref[...] = sums[...].astype(BF)
    n = own_ref.shape[0]
    own_ref[...] = sums[pl.ds(pl.multiple_of(x_at_ref[0] * n, n), n), :]


def down(x_at, h, w):
    n, hidden = h.shape
    return pl.pallas_call(
        down_kernel,
        out_shape=[jax.ShapeDtypeStruct((n, w.shape[1]), BF), jax.ShapeDtypeStruct((n // (32 // NB), w.shape[1]), F32)],
        in_specs=[SMEM, VMEM, VMEM],
        out_specs=[VMEM, VMEM],
        scratch_shapes=[pltpu.VMEM((n, w.shape[1]), F32)],
        cost_estimate=pl.CostEstimate(flops=2 * n * hidden * w.shape[1], bytes_accessed=4 << 20, transcendentals=0),
        compiler_params=pltpu.CompilerParams(vmem_limit_bytes=16 << 20),
        name="down",
    )(x_at, h, w)


def on_device(tokens, gate_weight, up_weight, down_weight):
    rows, width = tokens.shape
    hidden_units = gate_weight.shape[1]
    place = {a: lax.axis_index(a).astype(jnp.int32) for a in ("y", "c", "x", ZB)}
    place["xa"] = place["x"] * 2 + lax.axis_index("zp") if ZSPLIT else place["x"]
    far_from = {a: [place[a] != i for i in range(n)] for a, n in (("y", 4), ("xa", 32 // NB), (ZB, NB))}
    core, first = place["c"].reshape(1), place["c"] == 0
    place, far_from, core, other_core, first, tokens = lax.optimization_barrier(
        (place, far_from, core, 1 - core, first, tokens)
    )
    piece = gather(tokens, ZB, NB).reshape(NB * rows, width)
    piece = gather(piece, XA, 32 // NB).reshape(4, 2, 4 * rows, width)

    other = gate_up(other_core, piece, gate_weight.T, up_weight.T)
    other = lax.ppermute(other, "c", SWAP)
    mine = gate_up(core, piece, gate_weight.T, up_weight.T)
    y = place["y"]
    summed = scatter_sum((mine + other).astype(BF), "y", far_from["y"], at(mine, y) + at(other, y))
    summed = summed + lax.ppermute(summed.astype(BF), "zh", SWAP).astype(F32)

    hidden = (jax.nn.silu(summed[:, :hidden_units]) * summed[:, hidden_units:]).astype(BF)
    hidden = gather(hidden, "y", 4)
    far = lax.ppermute(hidden, "c", SWAP)
    hidden = jnp.stack([jnp.where(first, hidden, far), jnp.where(first, far, hidden)], axis=1)
    hidden = hidden.reshape(32 * rows, hidden_units)

    out, own = down(place["xa"].reshape(1), hidden, down_weight)
    out = scatter_sum(out.reshape(32 // NB, NB * rows, width), XA, far_from["xa"], own)
    out = out.reshape(NB, rows, width)
    out = scatter_sum(out.astype(BF), ZB, far_from[ZB], at(out, place[ZB]))
    return out.astype(BF)


def solution(mesh):
    sizes = [n for _, n in GX + GY]
    names = [a for a, _ in GX + GY]
    fine = Mesh(mesh.devices.reshape(sizes), names)
    gx, gy = tuple(a for a, _ in GX), tuple(a for a, _ in GY)
    return jax.shard_map(
        on_device,
        mesh=fine,
        in_specs=(P(gy, gx), P(gx, gy), P(gx, gy), P(gy, gx)),
        out_specs=P(gy, gx),
        check_vma=False,
    )
```

```python
import jax
import jax.numpy as jnp
from jax import lax
from jax.experimental import pallas as pl
from jax.experimental.pallas import tpu as pltpu
from jax.sharding import Mesh, PartitionSpec as P


GX = (("y", 4), ("zh", 2), ("c", 2))
GY = (("x", 4), ("zq", 4), ("zp", 2))
NEAR = ("x", "zp")
FAR = ("zq", "c")
BF = jnp.bfloat16
F32 = jnp.float32
LAST = BF
SWAP = [(0, 1), (1, 0)]
VMEM = pl.BlockSpec(memory_space=pltpu.VMEM)
SMEM = pl.BlockSpec(memory_space=pltpu.SMEM)
HBM = pl.BlockSpec(memory_space=pltpu.HBM)


def params(mib):
    return pltpu.CompilerParams(vmem_limit_bytes=mib << 20)


def add_far(parts, far, own):
    for i, is_far in enumerate(far):
        own = own + jnp.where(is_far, parts[i].astype(F32), 0.0)
    return own


def gate_up_kernel(place_ref, x_ref, *refs):
    weights, (out_ref, own_ref, sums, held, arrived) = refs[:4], refs[4:]
    copies = [pltpu.make_async_copy(w, held.at[i], arrived.at[i]) for i, w in enumerate(weights)]
    for copy in copies:
        copy.start()
    n_y, rows, _ = out_ref.shape
    blocks, _, block, width = x_ref.shape
    core = place_ref[0]
    near = x_ref[:, core].reshape(blocks * block, width)
    far = x_ref[:, 1 - core].reshape(blocks * block, width)
    dims = (((1,), (1,)), ((), ()))
    for i in range(2):
        copies[2 * i].wait()
        part = lax.dot_general(near, held[2 * i], dims, preferred_element_type=F32)
        copies[2 * i + 1].wait()
        part = part + lax.dot_general(far, held[2 * i + 1], dims, preferred_element_type=F32)
        n = part.shape[1]
        part = part.reshape(n_y, rows, n)
        sums[:, :, i * n : (i + 1) * n] = part
        out_ref[:, :, i * n : (i + 1) * n] = part.astype(BF)
    own_ref[...] = sums[place_ref[1]]


def gate_up(place, x, g, g2, u, u2):
    blocks, _, block, width = x.shape
    hidden = g.shape[0]
    shape = (4, blocks * block // 4, 2 * hidden)
    return pl.pallas_call(
        gate_up_kernel,
        out_shape=[jax.ShapeDtypeStruct(shape, BF), jax.ShapeDtypeStruct(shape[1:], F32)],
        in_specs=[SMEM, VMEM] + [HBM] * 4,
        out_specs=[VMEM, VMEM],
        scratch_shapes=[
            pltpu.VMEM(shape, F32),
            pltpu.VMEM((4,) + g.shape, BF),
            pltpu.SemaphoreType.DMA((4,)),
        ],
        cost_estimate=pl.CostEstimate(flops=8 * blocks * block * width * hidden, bytes_accessed=10 << 20, transcendentals=0),
        compiler_params=params(50),
        name="gate_up",
    )(place, x, g, g2, u, u2)


def hidden_kernel(near_ref, far_ref, out_ref):
    total = near_ref[...] + far_ref[...].astype(F32)
    n = out_ref.shape[2]
    gate, up = total[:, :n], total[:, n:]
    value = (gate / (1.0 + jnp.exp(-gate)) * up).astype(BF)
    for i in range(out_ref.shape[0]):
        out_ref[i] = value


def hidden_copies(near, far, copies):
    rows, width = near.shape
    return pl.pallas_call(
        hidden_kernel,
        out_shape=jax.ShapeDtypeStruct((copies, rows, width // 2), BF),
        in_specs=[VMEM, VMEM],
        out_specs=VMEM,
        cost_estimate=pl.CostEstimate(flops=8 * rows * width, bytes_accessed=1 << 20, transcendentals=rows * width),
        compiler_params=params(8),
        name="hidden",
    )(near, far)


def down_kernel(place_ref, h_ref, w_ref, w2_ref, out_ref, own_ref, sums):
    blocks, _, block, width = out_ref.shape
    h = h_ref[...].reshape(blocks * block, h_ref.shape[2])
    for w, half in ((w_ref, place_ref[0]), (w2_ref, 1 - place_ref[0])):
        part = jnp.dot(h, w[...], preferred_element_type=F32).reshape(blocks, block, width)
        sums[:, half] = part
        out_ref[:, half] = part.astype(BF)
    own_ref[...] = sums[place_ref[2]]


def down(place, h, w, w2):
    hidden, width = w.shape
    rows = h.shape[0] * h.shape[1]
    shape = (8, 2, rows // 8, width)
    return pl.pallas_call(
        down_kernel,
        out_shape=[jax.ShapeDtypeStruct(shape, BF), jax.ShapeDtypeStruct(shape[1:], F32)],
        in_specs=[SMEM, VMEM, VMEM, VMEM],
        out_specs=[VMEM, VMEM],
        scratch_shapes=[pltpu.VMEM(shape, F32)],
        cost_estimate=pl.CostEstimate(flops=4 * rows * hidden * width, bytes_accessed=6 << 20, transcendentals=0),
        compiler_params=params(20),
        name="down",
    )(place, h, w, w2)


def block(tokens, gate_weight, up_weight, down_weight):
    rows, width = tokens.shape
    half = rows // 2
    at = {a: lax.axis_index(a).astype(jnp.int32) for a in ("y", "c", "x", "zp", "zq")}
    near, far = at["x"] * 2 + at["zp"], at["zq"] * 2 + at["c"]
    place = jnp.stack([at["c"], at["y"], near])
    far_y = [at["y"] != i for i in range(4)]
    far_near = [near != i for i in range(8)]
    mine = [at["c"] == i for i in range(2)]
    far_zq = [[(far != 2 * q + i) for q in range(4)] for i in range(2)]
    at, place, far_y, far_near, mine, far_zq, tokens = lax.optimization_barrier(
        (at, place, far_y, far_near, mine, far_zq, tokens)
    )

    gate_weight, up_weight = gate_weight.T, up_weight.T
    gate_other = lax.ppermute(gate_weight, "c", SWAP)
    up_other = lax.ppermute(up_weight, "c", SWAP)
    piece = jnp.broadcast_to(tokens.reshape(1, 2, half, width), (4, 2, half, width))
    piece = lax.all_to_all(piece.reshape(8, half, width), FAR, 0, 0).reshape(4, 2, half, width)
    piece = piece.transpose(1, 0, 2, 3).reshape(1, 2, 4 * half, width)
    piece = lax.all_to_all(jnp.broadcast_to(piece, (8, 2, 4 * half, width)), NEAR, 0, 0)

    parts, own = gate_up(place, piece, gate_weight, gate_other, up_weight, up_other)
    parts, own = lax.optimization_barrier((parts, own))
    summed = add_far(lax.all_to_all(parts, "y", 0, 0), far_y, own)
    rounded = summed.astype(BF)
    rounded, down_weight = lax.optimization_barrier((rounded, down_weight))
    other = lax.ppermute(rounded, "zh", SWAP)
    down_other = lax.ppermute(down_weight, "c", SWAP)
    hidden = lax.all_to_all(hidden_copies(summed, other, 4), "y", 0, 0)

    parts, own = down(place, hidden, down_weight, down_other)
    parts, own = lax.optimization_barrier((parts, own))
    out = add_far(lax.all_to_all(parts, NEAR, 0, 0), far_near, own)

    out = out.reshape(2, 4, half, width).transpose(1, 0, 2, 3)
    own = lax.dynamic_index_in_dim(out, at["zq"], 0, keepdims=False, allow_negative_indices=False)
    parts = out.astype(LAST).reshape(8, half, width)
    own = jnp.where(mine[0], own[0], own[1])
    parts, own = lax.optimization_barrier((parts, own))
    parts = lax.all_to_all(parts, FAR, 0, 0).reshape(4, 2, half, width)
    halves = [
        add_far(parts[:, i], far_zq[i], jnp.where(mine[i], own, 0.0)).astype(BF) for i in range(2)
    ]
    return jnp.concatenate(halves, axis=0)


def solution(mesh):
    sizes = [n for _, n in GX + GY]
    names = [a for a, _ in GX + GY]
    fine = Mesh(mesh.devices.reshape(sizes), names)
    gx, gy = tuple(a for a, _ in GX), tuple(a for a, _ in GY)
    return jax.shard_map(
        block,
        mesh=fine,
        in_specs=(P(gy, gx), P(gx, gy), P(gx, gy), P(gy, gx)),
        out_specs=P(gy, gx),
        check_vma=False,
    )
```

```python
import jax
import jax.numpy as jnp
from jax import lax
from jax.experimental import pallas as pl
from jax.experimental.pallas import tpu as pltpu
from jax.sharding import Mesh, PartitionSpec as P


GX = (("y", 4), ("zh", 2), ("c", 2))
GY = (("x", 4), ("zq", 4), ("zp", 2))
NEAR = ("x", "zp")
FAR = ("zq", "c")
BF = jnp.bfloat16
F32 = jnp.float32
LAST = BF
SWAP = [(0, 1), (1, 0)]
VMEM = pl.BlockSpec(memory_space=pltpu.VMEM)
SMEM = pl.BlockSpec(memory_space=pltpu.SMEM)


def params(mib):
    return pltpu.CompilerParams(vmem_limit_bytes=mib << 20)


def add_far(parts, far, own):
    for i, is_far in enumerate(far):
        own = own + jnp.where(is_far, parts[i].astype(F32), 0.0)
    return own


def gate_up_kernel(place_ref, x_ref, g_ref, u_ref, g2_ref, u2_ref, out_ref, own_ref, sums):
    n_y, rows, _ = out_ref.shape
    blocks, _, block, width = x_ref.shape
    core = place_ref[0]
    near = x_ref[:, core].reshape(blocks * block, width)
    far = x_ref[:, 1 - core].reshape(blocks * block, width)
    dims = (((1,), (1,)), ((), ()))
    for i, (w, w2) in enumerate(((g_ref, g2_ref), (u_ref, u2_ref))):
        part = lax.dot_general(near, w[...], dims, preferred_element_type=F32)
        part = part + lax.dot_general(far, w2[...], dims, preferred_element_type=F32)
        n = part.shape[1]
        part = part.reshape(n_y, rows, n)
        sums[:, :, i * n : (i + 1) * n] = part
        out_ref[:, :, i * n : (i + 1) * n] = part.astype(BF)
    own_ref[...] = sums[place_ref[1]]


def gate_up(place, x, g, u, g2, u2):
    blocks, _, block, width = x.shape
    hidden = g.shape[0]
    shape = (4, blocks * block // 4, 2 * hidden)
    return pl.pallas_call(
        gate_up_kernel,
        out_shape=[jax.ShapeDtypeStruct(shape, BF), jax.ShapeDtypeStruct(shape[1:], F32)],
        in_specs=[SMEM] + [VMEM] * 5,
        out_specs=[VMEM, VMEM],
        scratch_shapes=[pltpu.VMEM(shape, F32)],
        cost_estimate=pl.CostEstimate(flops=8 * blocks * block * width * hidden, bytes_accessed=10 << 20, transcendentals=0),
        compiler_params=params(20),
        name="gate_up",
    )(place, x, g, u, g2, u2)


def hidden_kernel(near_ref, far_ref, out_ref):
    total = near_ref[...] + far_ref[...].astype(F32)
    n = out_ref.shape[2]
    gate, up = total[:, :n], total[:, n:]
    value = (gate / (1.0 + jnp.exp(-gate)) * up).astype(BF)
    for i in range(out_ref.shape[0]):
        out_ref[i] = value


def hidden_copies(near, far, copies):
    rows, width = near.shape
    return pl.pallas_call(
        hidden_kernel,
        out_shape=jax.ShapeDtypeStruct((copies, rows, width // 2), BF),
        in_specs=[VMEM, VMEM],
        out_specs=VMEM,
        cost_estimate=pl.CostEstimate(flops=8 * rows * width, bytes_accessed=1 << 20, transcendentals=rows * width),
        compiler_params=params(8),
        name="hidden",
    )(near, far)


def down_kernel(place_ref, h_ref, w_ref, w2_ref, out_ref, own_ref, sums):
    blocks, _, block, width = out_ref.shape
    h = h_ref[...].reshape(blocks * block, h_ref.shape[2])
    for w, half in ((w_ref, place_ref[0]), (w2_ref, 1 - place_ref[0])):
        part = jnp.dot(h, w[...], preferred_element_type=F32).reshape(blocks, block, width)
        sums[:, half] = part
        out_ref[:, half] = part.astype(BF)
    own_ref[...] = sums[place_ref[2]]


def down(place, h, w, w2):
    hidden, width = w.shape
    rows = h.shape[0] * h.shape[1]
    shape = (8, 2, rows // 8, width)
    return pl.pallas_call(
        down_kernel,
        out_shape=[jax.ShapeDtypeStruct(shape, BF), jax.ShapeDtypeStruct(shape[1:], F32)],
        in_specs=[SMEM, VMEM, VMEM, VMEM],
        out_specs=[VMEM, VMEM],
        scratch_shapes=[pltpu.VMEM(shape, F32)],
        cost_estimate=pl.CostEstimate(flops=4 * rows * hidden * width, bytes_accessed=6 << 20, transcendentals=0),
        compiler_params=params(20),
        name="down",
    )(place, h, w, w2)


def block(tokens, gate_weight, up_weight, down_weight):
    rows, width = tokens.shape
    half = rows // 2
    at = {a: lax.axis_index(a).astype(jnp.int32) for a in ("y", "c", "x", "zp", "zq")}
    near, far = at["x"] * 2 + at["zp"], at["zq"] * 2 + at["c"]
    place = jnp.stack([at["c"], at["y"], near])
    far_y = [at["y"] != i for i in range(4)]
    far_near = [near != i for i in range(8)]
    mine = [at["c"] == i for i in range(2)]
    far_zq = [[(far != 2 * q + i) for q in range(4)] for i in range(2)]
    at, place, far_y, far_near, mine, far_zq, tokens = lax.optimization_barrier(
        (at, place, far_y, far_near, mine, far_zq, tokens)
    )

    gate_weight, up_weight = gate_weight.T, up_weight.T
    gate_other = lax.ppermute(gate_weight, "c", SWAP)
    up_other = lax.ppermute(up_weight, "c", SWAP)
    piece = jnp.broadcast_to(tokens.reshape(1, 2, half, width), (4, 2, half, width))
    piece = lax.all_to_all(piece.reshape(8, half, width), FAR, 0, 0)
    piece = piece.reshape(4, 2, half, width)
    piece, gate_other, up_other = lax.optimization_barrier((piece, gate_other, up_other))
    piece = piece.transpose(1, 0, 2, 3).reshape(1, 2, 4 * half, width)
    piece = jnp.broadcast_to(piece, (8, 2, 4 * half, width))
    piece = lax.all_to_all(piece, NEAR, 0, 0)

    parts, own = gate_up(place, piece, gate_weight, up_weight, gate_other, up_other)
    parts, own = lax.optimization_barrier((parts, own))
    summed = add_far(lax.all_to_all(parts, "y", 0, 0), far_y, own)
    rounded = summed.astype(BF)
    rounded, down_weight = lax.optimization_barrier((rounded, down_weight))
    other = lax.ppermute(rounded, "zh", SWAP)
    down_other = lax.ppermute(down_weight, "c", SWAP)
    hidden = lax.all_to_all(hidden_copies(summed, other, 4), "y", 0, 0)

    parts, own = down(place, hidden, down_weight, down_other)
    parts, own = lax.optimization_barrier((parts, own))
    out = add_far(lax.all_to_all(parts, NEAR, 0, 0), far_near, own)

    out = out.reshape(2, 4, half, width).transpose(1, 0, 2, 3)
    own = lax.dynamic_index_in_dim(out, at["zq"], 0, keepdims=False, allow_negative_indices=False)
    parts = out.astype(LAST).reshape(8, half, width)
    own = jnp.where(mine[0], own[0], own[1])
    parts, own = lax.optimization_barrier((parts, own))
    parts = lax.all_to_all(parts, FAR, 0, 0).reshape(4, 2, half, width)
    halves = [
        add_far(parts[:, i], far_zq[i], jnp.where(mine[i], own, 0.0)).astype(BF) for i in range(2)
    ]
    return jnp.concatenate(halves, axis=0)


def solution(mesh):
    sizes = [n for _, n in GX + GY]
    names = [a for a, _ in GX + GY]
    fine = Mesh(mesh.devices.reshape(sizes), names)
    gx, gy = tuple(a for a, _ in GX), tuple(a for a, _ in GY)
    return jax.shard_map(
        block,
        mesh=fine,
        in_specs=(P(gy, gx), P(gx, gy), P(gx, gy), P(gy, gx)),
        out_specs=P(gy, gx),
        check_vma=False,
    )
```

```python
import jax
import jax.numpy as jnp
from jax import lax
from jax.experimental import pallas as pl
from jax.experimental.pallas import tpu as pltpu
from jax.sharding import Mesh, PartitionSpec as P


GX = (("y", 4), ("zh", 2), ("c", 2))
GY = (("x", 4), ("zq", 4), ("zp", 2))
NEAR = ("x", "zp")
FAR = ("zq", "c")
BF = jnp.bfloat16
F32 = jnp.float32
LAST = BF
SWAP = [(0, 1), (1, 0)]
PIECES = 4
VMEM = pl.BlockSpec(memory_space=pltpu.VMEM)
SMEM = pl.BlockSpec(memory_space=pltpu.SMEM)
FREE = pl.BlockSpec(memory_space=pl.ANY)


def params(mib):
    return pltpu.CompilerParams(vmem_limit_bytes=mib << 20)


def add_far(parts, far, own):
    for i, is_far in enumerate(far):
        own = own + jnp.where(is_far, parts[i].astype(F32), 0.0)
    return own


def gate_up_kernel(place_ref, x_ref, *refs):
    weights, (out_ref, own_ref, sums, held, arrived) = refs[:4], refs[4:]
    n = weights[0].shape[0]
    cuts = [(j * n // PIECES, (j + 1) * n // PIECES) for j in range(PIECES)]
    copies = [
        [
            pltpu.make_async_copy(w.at[i:j], held.at[at, i:j], arrived.at[at, piece])
            for piece, (i, j) in enumerate(cuts)
        ]
        for at, w in enumerate(weights)
    ]
    for at in (0, 2, 1, 3):
        for copy in copies[at]:
            copy.start()
    n_y, rows, _ = out_ref.shape
    blocks, _, block, width = x_ref.shape
    core = place_ref[0]
    dims = (((1,), (1,)), ((), ()))

    def products(features, at):
        for copy in copies[at]:
            copy.wait()
        x = x_ref[:, features].reshape(blocks * block, width)
        return lax.dot_general(x, held[at], dims, preferred_element_type=F32).reshape(n_y, rows, n)

    for i in range(2):
        part = products(core, i) + products(1 - core, 2 + i)
        sums[:, :, i * n : (i + 1) * n] = part
        out_ref[:, :, i * n : (i + 1) * n] = part.astype(BF)
    own_ref[...] = sums[place_ref[1]]


def gate_up(place, x, g, u, g2, u2):
    blocks, _, block, width = x.shape
    hidden = g.shape[0]
    shape = (4, blocks * block // 4, 2 * hidden)
    return pl.pallas_call(
        gate_up_kernel,
        out_shape=[jax.ShapeDtypeStruct(shape, BF), jax.ShapeDtypeStruct(shape[1:], F32)],
        in_specs=[SMEM, VMEM] + [FREE] * 4,
        out_specs=[VMEM, VMEM],
        scratch_shapes=[
            pltpu.VMEM(shape, F32),
            pltpu.VMEM((4,) + g.shape, BF),
            pltpu.SemaphoreType.DMA((4, PIECES)),
        ],
        cost_estimate=pl.CostEstimate(flops=8 * blocks * block * width * hidden, bytes_accessed=10 << 20, transcendentals=0),
        compiler_params=params(50),
        name="gate_up",
    )(place, x, g, u, g2, u2)


def hidden_kernel(near_ref, far_ref, out_ref):
    total = near_ref[...] + far_ref[...].astype(F32)
    n = out_ref.shape[2]
    gate, up = total[:, :n], total[:, n:]
    value = (gate / (1.0 + jnp.exp(-gate)) * up).astype(BF)
    for i in range(out_ref.shape[0]):
        out_ref[i] = value


def hidden_copies(near, far, copies):
    rows, width = near.shape
    return pl.pallas_call(
        hidden_kernel,
        out_shape=jax.ShapeDtypeStruct((copies, rows, width // 2), BF),
        in_specs=[VMEM, VMEM],
        out_specs=VMEM,
        cost_estimate=pl.CostEstimate(flops=8 * rows * width, bytes_accessed=1 << 20, transcendentals=rows * width),
        compiler_params=params(8),
        name="hidden",
    )(near, far)


def down_kernel(place_ref, h_ref, w_ref, w2_ref, out_ref, own_ref, sums):
    blocks, _, block, width = out_ref.shape
    h = h_ref[...].reshape(blocks * block, h_ref.shape[2])
    for w, half in ((w_ref, place_ref[0]), (w2_ref, 1 - place_ref[0])):
        part = jnp.dot(h, w[...], preferred_element_type=F32).reshape(blocks, block, width)
        sums[:, half] = part
        out_ref[:, half] = part.astype(BF)
    own_ref[...] = sums[place_ref[2]]


def down(place, h, w, w2):
    hidden, width = w.shape
    rows = h.shape[0] * h.shape[1]
    shape = (8, 2, rows // 8, width)
    return pl.pallas_call(
        down_kernel,
        out_shape=[jax.ShapeDtypeStruct(shape, BF), jax.ShapeDtypeStruct(shape[1:], F32)],
        in_specs=[SMEM, VMEM, VMEM, VMEM],
        out_specs=[VMEM, VMEM],
        scratch_shapes=[pltpu.VMEM(shape, F32)],
        cost_estimate=pl.CostEstimate(flops=4 * rows * hidden * width, bytes_accessed=6 << 20, transcendentals=0),
        compiler_params=params(20),
        name="down",
    )(place, h, w, w2)


def block(tokens, gate_weight, up_weight, down_weight):
    rows, width = tokens.shape
    half = rows // 2
    at = {a: lax.axis_index(a).astype(jnp.int32) for a in ("y", "c", "x", "zp", "zq")}
    near, far = at["x"] * 2 + at["zp"], at["zq"] * 2 + at["c"]
    place = jnp.stack([at["c"], at["y"], near])
    far_y = [at["y"] != i for i in range(4)]
    far_near = [near != i for i in range(8)]
    mine = [at["c"] == i for i in range(2)]
    far_zq = [[(far != 2 * q + i) for q in range(4)] for i in range(2)]
    at, place, far_y, far_near, mine, far_zq, tokens = lax.optimization_barrier(
        (at, place, far_y, far_near, mine, far_zq, tokens)
    )

    gate_weight, up_weight = gate_weight.T, up_weight.T
    gate_other = lax.ppermute(gate_weight, "c", SWAP)
    up_other = lax.ppermute(up_weight, "c", SWAP)
    piece = jnp.broadcast_to(tokens.reshape(1, 2, half, width), (4, 2, half, width))
    piece = lax.all_to_all(piece.reshape(8, half, width), FAR, 0, 0)
    piece = piece.reshape(4, 2, half, width)
    piece = piece.transpose(1, 0, 2, 3).reshape(1, 2, 4 * half, width)
    piece = jnp.broadcast_to(piece, (8, 2, 4 * half, width))
    piece = lax.all_to_all(piece, NEAR, 0, 0)

    parts, own = gate_up(place, piece, gate_weight, up_weight, gate_other, up_other)
    parts, own = lax.optimization_barrier((parts, own))
    summed = add_far(lax.all_to_all(parts, "y", 0, 0), far_y, own)
    rounded = summed.astype(BF)
    rounded, down_weight = lax.optimization_barrier((rounded, down_weight))
    other = lax.ppermute(rounded, "zh", SWAP)
    down_other = lax.ppermute(down_weight, "c", SWAP)
    hidden = lax.all_to_all(hidden_copies(summed, other, 4), "y", 0, 0)

    parts, own = down(place, hidden, down_weight, down_other)
    parts, own = lax.optimization_barrier((parts, own))
    out = add_far(lax.all_to_all(parts, NEAR, 0, 0), far_near, own)

    out = out.reshape(2, 4, half, width).transpose(1, 0, 2, 3)
    own = lax.dynamic_index_in_dim(out, at["zq"], 0, keepdims=False, allow_negative_indices=False)
    parts = out.astype(LAST).reshape(8, half, width)
    own = jnp.where(mine[0], own[0], own[1])
    parts, own = lax.optimization_barrier((parts, own))
    parts = lax.all_to_all(parts, FAR, 0, 0).reshape(4, 2, half, width)
    halves = [
        add_far(parts[:, i], far_zq[i], jnp.where(mine[i], own, 0.0)).astype(BF) for i in range(2)
    ]
    return jnp.concatenate(halves, axis=0)


def solution(mesh):
    sizes = [n for _, n in GX + GY]
    names = [a for a, _ in GX + GY]
    fine = Mesh(mesh.devices.reshape(sizes), names)
    gx, gy = tuple(a for a, _ in GX), tuple(a for a, _ in GY)
    return jax.shard_map(
        block,
        mesh=fine,
        in_specs=(P(gy, gx), P(gx, gy), P(gx, gy), P(gy, gx)),
        out_specs=P(gy, gx),
        check_vma=False,
    )
```
